32 devices in a mesh: ctx: 8 (over y, x, core), fsdp: 4 (over z).
Axes of the slice: x: 2, y: 2, z: 4, core: 2. Of those that a mesh axis runs over, the one named last changes fastest.
Arguments:
- loaded: bfloat16 [8, 8, 128, 4096], P('ctx', None, None, 'fsdp'), may hold values from -6 to 6
- slot_pos: int32 [8, 8, 128], P('ctx'), may hold values from -1 to 255, as said below
- contig_lengths: int32 [16], replicated, may hold values from 1 to 1024, 2048 in all
- w_in: bfloat16 [4096, 3, 4096], P('ctx', None, 'fsdp'), may hold values from -0.09375 to 0.09375
- short_taps: float32 [3, 7, 4096], P(None, None, 'fsdp'), may hold values from -2 to 2
- long_taps: float32 [128, 4096], P(None, 'fsdp'), may hold values from -0.5 to 0.5
- grad_out: bfloat16 [2048, 4096], P('ctx', 'fsdp'), may hold values from -0.59765625 to 0.59765625
Outputs:
- gated_out: bfloat16 [2048, 4096], P('ctx', 'fsdp')
- token_grads: bfloat16 [2048, 4096], P('ctx', 'fsdp')
- weight_grads: bfloat16 [4096, 3, 4096], P('ctx', None, 'fsdp')
- short_grads: float32 [3, 7, 4096], P(None, None, 'fsdp')
- long_grads: float32 [128, 4096], P(None, 'fsdp')
The draws below stay inside these ranges and needn't reach their ends.
Inputs may be any that keep to these rules, and one draw needn't show every extreme that they name: `slot_pos`: for each destination e, the slots with a value of 0 or more name every row 0 to 255 of e's block exactly once; -1 marks an empty slot; for each destination some loader fills all 128 of its slots. `contig_lengths`: the lengths sum to 2048.
All inputs are finite; a program needn't handle non-finite values.
Results may differ from the reference program's by a relative error of at most 0.012.
Values may be sent and summed in bfloat16 or wider, within the bound.
A program may use at most 192 MiB of HBM per device.

```python
import math
import jax
import jax.numpy as jnp
import numpy as np
from jax import lax

D = 4096
HC = 4096
SHORT = 7
LONG = 128
TOK_DEV = 256
TOKENS = 2048
SLOT = 128
NCONTIG = 16
N_CTX = 8


def draw_slot_pos(key, part):
    groups = TOK_DEV // 8
    seats = SLOT // 8
    seat_total = N_CTX * seats
    dest_keys = jax.random.split(jax.random.fold_in(key, 11), N_CTX)

    def one_dest(dest_key):
        heavy_key, order_key, place_key = jax.random.split(dest_key, 3)
        heavy = jax.random.randint(heavy_key, (), 0, N_CTX)
        ranks = jax.random.permutation(order_key, seat_total).astype(jnp.int32)
        seat_ids = jnp.arange(seat_total, dtype=jnp.int32)
        owners = seat_ids // seats
        scores = jnp.where(owners == heavy, 0, seat_total) + ranks
        chosen = jnp.argsort(scores, stable=True)[:groups]
        placed = jax.random.permutation(place_key, groups).astype(jnp.int32)
        values = placed[:, None] * 8 + jnp.arange(8, dtype=jnp.int32)[None, :]
        table = jnp.full((seat_total, 8), -1, jnp.int32).at[chosen].set(values)
        return table.reshape(N_CTX, SLOT)
    return jax.vmap(one_dest)(dest_keys).astype(jnp.int32)


def steps_of(key, dims, cuts, least, high):
    loudness = 1.0
    for position, shards_of in cuts:
        heights = jax.random.uniform(jax.random.fold_in(jax.random.fold_in(key, 6), position), (shards_of,), jnp.float32, least / len(cuts), high / len(cuts))
        loudness = loudness * jnp.repeat(jnp.exp(heights), dims[position] // shards_of).reshape((-1,) + (1,) * (len(dims) - 1 - position))
    return loudness


def length_profile(count, total, bound, lean):
    weights = [(1 << 20) // math.isqrt(grade ** lean) + 1 for grade in range(2, count + 1)]
    surplus, counts = total - bound - (count - 1), [1] * (count - 1)
    while surplus > 0:
        free = [i for i in range(count - 1) if counts[i] < bound]
        mass, budget = sum([weights[i] for i in free]), surplus
        for i in free:
            extra = min(bound - counts[i], max(1, budget * weights[i] // mass), surplus)
            counts[i] = counts[i] + extra
            surplus = surplus - extra
    return np.array([bound] + counts)


def uneven(own_key, number_of, total, limit, lean):
    if number_of == 2:
        one = jax.random.randint(own_key, (), max(1, total - limit), min(limit, total - 1) + 1)
        return jnp.stack([one, total - one])
    lengths = jnp.asarray(length_profile(number_of, total, limit, lean), jnp.int32)
    pairs = (number_of - 1) // 2
    source_of, receiver = lengths[1:1 + 2 * pairs:2], lengths[2:2 + 2 * pairs:2]
    room = jnp.minimum(source_of - 1, limit - receiver)
    passed = jax.random.randint(jax.random.fold_in(own_key, 1), (pairs,), 0, 1 << 20) % (room + 1)
    lengths = lengths.at[1:1 + 2 * pairs:2].set(source_of - passed).at[2:2 + 2 * pairs:2].set(receiver + passed)
    return lengths[jax.random.permutation(jax.random.fold_in(own_key, 2), number_of)]


def normal_values(stream_key, shape, scale, limit, cuts=(), kind=jnp.bfloat16):
    level = steps_of(stream_key, shape, cuts, -0.22, 0.18) if cuts else 1.0
    result = jax.random.normal(stream_key, shape, jnp.float32) * scale * level
    return jnp.minimum(jnp.maximum(result, -limit), limit).astype(kind)


def setup_inputs(seed: int = 0) -> dict:
    keys = jax.random.split(jax.random.key(seed), 8)
    loaded = normal_values(keys[0], (N_CTX, N_CTX, SLOT, D), 1.0, 6.0, ((0, 8), (3, 4)))
    slot_pos = draw_slot_pos(jax.random.fold_in(keys[7], 71), 0)
    contig_lengths = uneven(keys[2], NCONTIG, TOKENS, 4 * TOK_DEV, 2).astype(jnp.int32)
    w_in = normal_values(keys[3], (D, 3, HC), D ** -0.5, 0.09375, ((0, 8), (2, 4)))
    short_taps = normal_values(keys[4], (3, SHORT, HC), SHORT ** -0.5, 2.0, ((2, 4),), jnp.float32)
    long_taps = normal_values(keys[5], (LONG, HC), LONG ** -0.5, 0.5, ((1, 4),), jnp.float32)
    grad_out = normal_values(keys[6], (TOKENS, HC), 0.1, 0.59765625, ((0, 8), (1, 4)))
    return {"loaded": loaded, "slot_pos": slot_pos, "contig_lengths": contig_lengths, "w_in": w_in, "short_taps": short_taps, "long_taps": long_taps, "grad_out": grad_out}


def starts_of(positions, contig_lengths):
    ends = jnp.cumsum(contig_lengths, dtype=jnp.int32)
    begins = ends - contig_lengths
    chosen = jnp.where(begins[None, :] <= positions[:, None], begins[None, :], 0)
    return jnp.max(chosen, axis=1).astype(jnp.int32)


def lead_filter(ext, taps, positions, begins_here):
    width = taps.shape[0]
    count = ext.shape[0] - width + 1
    bcast_shape = (count,) + (1,) * (ext.ndim - 1)
    total = jnp.zeros((count,) + ext.shape[1:], jnp.float32)
    for tap_index in range(width):
        keep_mask = (positions - tap_index >= begins_here).astype(jnp.float32).reshape(bcast_shape)
        first = width - 1 - tap_index
        total = total + taps[tap_index] * ext[first:first + count] * keep_mask
    return total


def trail_filter(ext, taps, positions, begins_ext):
    width = taps.shape[0]
    count = ext.shape[0] - width + 1
    bcast_shape = (count,) + (1,) * (ext.ndim - 1)
    total = jnp.zeros((count,) + ext.shape[1:], jnp.float32)
    for tap_index in range(width):
        keep_mask = (positions >= begins_ext[tap_index:tap_index + count]).astype(jnp.float32).reshape(bcast_shape)
        total = total + taps[tap_index] * ext[tap_index:tap_index + count] * keep_mask
    return total


def tap_sums(grads, ext, width, lead_count, positions, begins_here):
    count = grads.shape[0]
    bcast_shape = (count,) + (1,) * (grads.ndim - 1)
    pieces = []
    for tap_index in range(width):
        keep_mask = (positions - tap_index >= begins_here).astype(jnp.float32).reshape(bcast_shape)
        first = lead_count - tap_index
        pieces.append(jnp.sum(grads * ext[first:first + count] * keep_mask, axis=0))
    return jnp.stack(pieces, 0)


def reference(loaded, slot_pos, contig_lengths, w_in, short_taps, long_taps, grad_out):
    by_dest = jnp.transpose(loaded, (1, 0, 2, 3)).reshape(N_CTX * N_CTX * SLOT, D)
    bases = (jnp.arange(N_CTX, dtype=jnp.int32) * TOK_DEV)[:, None, None]
    targets = jnp.where(slot_pos >= 0, slot_pos + bases, TOKENS).reshape(-1).astype(jnp.int32)
    tokens = jnp.zeros((TOKENS, D), jnp.bfloat16).at[targets].set(by_dest, mode="drop")
    positions = jnp.arange(TOKENS, dtype=jnp.int32)
    begins_here = starts_of(positions, contig_lengths)
    long_begins = starts_of(jnp.arange(TOKENS + LONG - 1, dtype=jnp.int32), contig_lengths)
    short_begins = starts_of(jnp.arange(TOKENS + SHORT - 1, dtype=jnp.int32), contig_lengths)
    block_width = math.gcd(HC, 512)
    block_count = HC // block_width

    def channel_block(token_acc, block_index):
        start_col = (block_index * block_width).astype(jnp.int32)
        w_block = lax.dynamic_slice_in_dim(w_in, start_col, block_width, 2)
        flat_w = w_block.reshape(D, 3 * block_width)
        short_block = lax.dynamic_slice_in_dim(short_taps, start_col, block_width, 2)
        long_block = lax.dynamic_slice_in_dim(long_taps, start_col, block_width, 1)
        grad_block = lax.dynamic_slice_in_dim(grad_out, start_col, block_width, 1)
        streams = jnp.dot(tokens, flat_w, preferred_element_type=jnp.float32).reshape(TOKENS, 3, block_width)
        mixed_half = streams.astype(jnp.bfloat16)
        short_lags = jnp.transpose(short_block, (1, 0, 2))
        lead_mixed = jnp.concatenate([jnp.zeros((SHORT - 1, 3, block_width), jnp.bfloat16), mixed_half], 0).astype(jnp.float32)
        filtered = lead_filter(lead_mixed, short_lags, positions, begins_here)
        product = (filtered[:, 1] * filtered[:, 2]).astype(jnp.bfloat16)
        lead_product = jnp.concatenate([jnp.zeros((LONG - 1, block_width), jnp.bfloat16), product], 0).astype(jnp.float32)
        carried = lead_filter(lead_product, long_block, positions, begins_here)
        gated_block = (filtered[:, 0] * carried).astype(jnp.bfloat16)
        upstream = grad_block.astype(jnp.float32)
        back_prod = (upstream * filtered[:, 0]).astype(jnp.bfloat16)
        first_grad = upstream * carried
        trail_prod = jnp.concatenate([back_prod, jnp.zeros((LONG - 1, block_width), jnp.bfloat16)], 0).astype(jnp.float32)
        grad_product = trail_filter(trail_prod, long_block, positions, long_begins)
        grad_filtered = jnp.stack([first_grad, grad_product * filtered[:, 2], grad_product * filtered[:, 1]], 1).astype(jnp.bfloat16)
        trail_grad = jnp.concatenate([grad_filtered, jnp.zeros((SHORT - 1, 3, block_width), jnp.bfloat16)], 0).astype(jnp.float32)
        grad_mixed = trail_filter(trail_grad, short_lags, positions, short_begins).astype(jnp.bfloat16)
        flat_grad = grad_mixed.reshape(TOKENS, 3 * block_width)
        token_acc = token_acc + jnp.dot(flat_grad, flat_w.T, preferred_element_type=jnp.float32)

        def row_term(accum, row_block):
            start_row = (row_block * TOK_DEV).astype(jnp.int32)
            feature_rows = lax.dynamic_slice_in_dim(tokens, start_row, TOK_DEV, 0)
            grad_rows = lax.dynamic_slice_in_dim(flat_grad, start_row, TOK_DEV, 0)
            term = jnp.dot(feature_rows.T, grad_rows, preferred_element_type=jnp.float32).astype(jnp.bfloat16)
            return accum + lax.optimization_barrier(term).astype(jnp.float32), None

        summed, _ = lax.scan(row_term, jnp.zeros((D, 3 * block_width), jnp.float32), jnp.arange(N_CTX, dtype=jnp.int32))
        weight_block = summed.astype(jnp.bfloat16).reshape(D, 3, block_width)
        long_block_grads = tap_sums(back_prod.astype(jnp.float32), lead_product, LONG, LONG - 1, positions, begins_here)
        short_lag_grads = tap_sums(grad_filtered.astype(jnp.float32), lead_mixed, SHORT, SHORT - 1, positions, begins_here)
        short_block_grads = jnp.transpose(short_lag_grads, (1, 0, 2))
        return token_acc, (gated_block, weight_block, short_block_grads, long_block_grads)

    token_sum, outs = lax.scan(channel_block, jnp.zeros((TOKENS, D), jnp.float32), jnp.arange(block_count, dtype=jnp.int32))
    gated_blocks, weight_blocks, short_blocks, long_blocks = outs
    gated_out = jnp.transpose(gated_blocks, (1, 0, 2)).reshape(TOKENS, HC)
    weight_grads = jnp.transpose(weight_blocks, (1, 2, 0, 3)).reshape(D, 3, HC)
    short_grads = jnp.transpose(short_blocks, (1, 2, 0, 3)).reshape(3, SHORT, HC)
    long_grads = jnp.transpose(long_blocks, (1, 0, 2)).reshape(LONG, HC)
    token_grads = token_sum.astype(jnp.bfloat16)
    return gated_out, token_grads, weight_grads, short_grads, long_grads
```

```python
import jax
import jax.numpy as jnp
from jax import lax
from jax.experimental import pallas as pl
from jax.experimental.pallas import tpu as pltpu
from jax.sharding import PartitionSpec as P

LANES = 128


def round_up(x, to):
    return -(-x // to) * to


def neighbour_rows(x, axis, by):
    size = lax.axis_size(axis)
    pairs = [(i, i + by) for i in range(size) if 0 <= i + by < size]
    return lax.ppermute(x, axis, pairs)


def rotated(x, axis, by):
    size = lax.axis_size(axis)
    return lax.ppermute(x, axis, [(i, (i + by) % size) for i in range(size)])


def gather_by_permutes(x, axis, dim):
    size = lax.axis_size(axis)
    me = lax.axis_index(axis)
    width = x.shape[dim]
    shape = list(x.shape)
    shape[dim] = width * size
    out = lax.dynamic_update_slice_in_dim(jnp.zeros(shape, x.dtype), x, me * width, dim)
    for by in range(1, size):
        got = rotated(x, axis, by)
        out = lax.dynamic_update_slice_in_dim(out, got, ((me - by) % size) * width, dim)
    return out


def swap_by_permutes(x, axis, split_dim):
    size = lax.axis_size(axis)
    me = lax.axis_index(axis)
    width = x.shape[split_dim] // size
    pieces = [(me, lax.dynamic_slice_in_dim(x, me * width, width, split_dim))]
    for by in range(1, size):
        part = lax.dynamic_slice_in_dim(x, ((me + by) % size) * width, width, split_dim)
        pieces.append(((me - by) % size, rotated(part, axis, by)))
    return pieces


def summed_over(x, axis):
    size = lax.axis_size(axis)
    if size & (size - 1):
        return lax.psum(x.astype(jnp.bfloat16), axis).astype(jnp.float32)
    step = 1
    while step < size:
        mine = x.astype(jnp.bfloat16)
        got = lax.ppermute(mine, axis, [(i, i ^ step) for i in range(size)])
        x = mine.astype(jnp.float32) + got.astype(jnp.float32)
        step *= 2
    return x


def conv_kernel(
    dims, proj, prev12, prev0, next0, next12, grads, next_grads, dist, room, short, long,
    gated, mixed, long_sums, short_sums,
    s0, s1, s2, go, f0, f1, f2, prod, back, gf, acc,
):
    rows, lead, short_pad, short_w, long_w, tail = dims
    f32 = jnp.float32
    s0[0:short_pad, :] = prev0[...].astype(f32)
    s0[short_pad : short_pad + rows, :] = proj[0].astype(f32)
    s0[short_pad + rows :, :] = next0[...].astype(f32)
    for k, ref in ((0, s1), (1, s2)):
        ref[0 : lead + short_pad, :] = prev12[k].astype(f32)
        ref[lead + short_pad : lead + short_pad + rows, :] = proj[1 + k].astype(f32)
        ref[lead + short_pad + rows :, :] = next12[k].astype(f32)
    go[0:rows, :] = grads[...].astype(f32)
    go[rows:, :] = next_grads[...].astype(f32)

    def rounded(x):
        return x.astype(jnp.bfloat16).astype(f32)

    step = 8 * 7 if (lead + rows + tail) % 56 == 0 else 8

    def lead_short(ref, taps, base, reach, n):
        total = jnp.zeros((n, LANES), f32)
        for j in range(short_w):
            x = ref[pl.ds(base + short_pad - j, n), :]
            total = total + jnp.where(reach >= j, x, 0.0) * taps[j : j + 1, :]
        return total

    def before(i, _):
        base = pl.multiple_of(i * step, 8)
        reach = dist[pl.ds(base, step), :]
        a = lead_short(s1, short[1], base, reach, step)
        b = lead_short(s2, short[2], base, reach, step)
        f1[pl.ds(base, step), :] = a
        f2[pl.ds(base, step), :] = b
        prod[pl.ds(base, step), :] = rounded(a * b)
        return 0

    lax.fori_loop(0, (lead + rows + tail) // step, before, 0)

    def after(i, _):
        base = pl.multiple_of(i * step, 8)
        reach = dist[pl.ds(base + lead, step), :]
        a = lead_short(s0, short[0], base, reach, step)
        f0[pl.ds(base, step), :] = a
        back[pl.ds(base, step), :] = rounded(go[pl.ds(base, step), :] * a)
        return 0

    lax.fori_loop(0, (rows + tail + lead) // step, after, 0)

    acc[...] = jnp.zeros_like(acc)
    unroll = 8

    def long_tile(base, n, own):
        reach = dist[pl.ds(base + lead, n), :]
        ahead = room[pl.ds(base, n), :]
        here = back[pl.ds(base, n), :]

        def taps_step(i, carry):
            carried, grad = carry
            for u in range(unroll):
                j = i * unroll + u
                tap = long[pl.ds(j, 1), :]
                x = jnp.where(reach >= j, prod[pl.ds(base + lead - j, n), :], 0.0)
                y = jnp.where(ahead >= j, back[pl.ds(base + j, n), :], 0.0)
                carried = carried + x * tap
                grad = grad + y * tap
                if own:
                    z = here * x
                    part = z[0:8, :]
                    for r in range(8, n, 8):
                        part = part + z[r : r + 8, :]
                    at = pl.multiple_of(j * 8, 8)
                    acc[pl.ds(at, 8), :] += part
            return carried, grad

        zero = jnp.zeros((n, LANES), f32)
        carried, grad = lax.fori_loop(0, long_w // unroll, taps_step, (zero, zero))
        if own:
            gated[pl.ds(base, n), :] = (f0[pl.ds(base, n), :] * carried).astype(gated.dtype)
        gf[0, pl.ds(base, n), :] = rounded(go[pl.ds(base, n), :] * carried)
        gf[1, pl.ds(base, n), :] = rounded(grad * f2[pl.ds(base + lead, n), :])
        gf[2, pl.ds(base, n), :] = rounded(grad * f1[pl.ds(base + lead, n), :])

    tile = 64 if rows % 64 == 0 else 8
    lax.fori_loop(
        0, rows // tile, lambda i, _: (long_tile(pl.multiple_of(i * tile, 8), tile, True), 0)[1], 0
    )
    for extra in range(0, tail, 8):
        long_tile(rows + extra, 8, False)
    long_sums[...] = jnp.sum(acc[...].reshape(long_w, 8, LANES), axis=1)

    short_sums[...] = jnp.zeros_like(short_sums)

    def last(i, _):
        base = pl.multiple_of(i * tile, 8)
        reach = dist[pl.ds(base + lead, tile), :]
        ahead = room[pl.ds(base, tile), :]
        for s, ref, off in ((0, s0, 0), (1, s1, lead), (2, s2, lead)):
            total = jnp.zeros((tile, LANES), f32)
            here = gf[s, pl.ds(base, tile), :]
            for j in range(short_w):
                y = jnp.where(ahead >= j, gf[s, pl.ds(base + j, tile), :], 0.0)
                total = total + y * short[s, j : j + 1, :]
                x = jnp.where(reach >= j, ref[pl.ds(base + off + short_pad - j, tile), :], 0.0)
                short_sums[s, j : j + 1, :] += jnp.sum(here * x, axis=0, keepdims=True)
            mixed[s, pl.ds(base, tile), :] = total.astype(mixed.dtype)
        return 0

    lax.fori_loop(0, rows // tile, last, 0)


def conv_block(proj, grad_out, short_taps, long_taps, contig_lengths):
    _, rows, chans = proj.shape
    short_w, long_w = short_taps.shape[1], long_taps.shape[0]
    short_pad = 16
    lead = round_up(long_w, 16)
    tail = round_up(short_w - 1, 8)
    far = lead + short_pad

    up = neighbour_rows(proj[1:, rows - far :], "ctx", 1)
    up0 = neighbour_rows(proj[0, rows - short_pad :], "ctx", 1)
    down0 = neighbour_rows(proj[0, :far], "ctx", -1)
    down12 = neighbour_rows(proj[1:, :short_pad], "ctx", -1)
    down_grads = neighbour_rows(grad_out[:far], "ctx", -1)

    offset = lax.axis_index("ctx") * rows
    ends = jnp.cumsum(contig_lengths, dtype=jnp.int32)
    begins = ends - contig_lengths
    at = offset - lead + jnp.arange(lead + rows + far, dtype=jnp.int32)
    first = jnp.max(jnp.where(begins[None, :] <= at[:, None], begins[None, :], 0), axis=1)
    dist = jnp.broadcast_to((at - first)[:, None], (at.shape[0], LANES))
    here = offset + jnp.arange(rows + short_pad, dtype=jnp.int32)
    big = jnp.int32(2**30)
    end = jnp.min(jnp.where(ends[None, :] > here[:, None], ends[None, :], big), axis=1)
    room = jnp.broadcast_to((end - 1 - here)[:, None], (here.shape[0], LANES))

    def block(*lead_dims):
        n = len(lead_dims)
        return pl.BlockSpec((*lead_dims, LANES), lambda i: (0,) * n + (i,))

    def whole(r):
        return pl.BlockSpec((r, LANES), lambda i: (0, 0))

    def vmem(*shape):
        return pltpu.VMEM((*shape, LANES), jnp.float32)

    span = lead + rows + tail
    dims = (rows, lead, short_pad, short_w, long_w, tail)
    return pl.pallas_call(
        lambda *refs: conv_kernel(dims, *refs),
        grid=(chans // LANES,),
        in_specs=[
            block(3, rows), block(2, far), block(short_pad), block(far), block(2, short_pad),
            block(rows), block(far), whole(dist.shape[0]), whole(room.shape[0]),
            block(3, short_w), block(long_w),
        ],
        out_specs=[block(rows), block(3, rows), block(long_w), block(3, 8 * -(-short_w // 8))],
        out_shape=[
            jax.ShapeDtypeStruct((rows, chans), jnp.bfloat16),
            jax.ShapeDtypeStruct((3, rows, chans), jnp.bfloat16),
            jax.ShapeDtypeStruct((long_w, chans), jnp.float32),
            jax.ShapeDtypeStruct((3, 8 * -(-short_w // 8), chans), jnp.float32),
        ],
        scratch_shapes=[
            vmem(short_pad + rows + far), vmem(far + rows + short_pad),
            vmem(far + rows + short_pad), vmem(rows + far),
            vmem(span), vmem(span), vmem(span), vmem(span), vmem(span),
            vmem(3, rows + short_pad), vmem(long_w * 8),
        ],
        compiler_params=pltpu.CompilerParams(vmem_limit_bytes=40 << 20),
        cost_estimate=pl.CostEstimate(
            flops=rows * chans * long_w * 10, bytes_accessed=rows * chans * 24, transcendentals=0
        ),
        name="hyena_filters",
    )(proj, up, up0, down0, down12, grad_out, down_grads, dist, room, short_taps, long_taps)


def on_device(loaded, slot_pos, contig_lengths, w_in, short_taps, long_taps, grad_out):
    f32, bf16 = jnp.float32, jnp.bfloat16
    rows, chans = grad_out.shape
    short_w, long_w = short_taps.shape[1], long_taps.shape[0]
    weights = lax.all_gather(jnp.transpose(w_in, (1, 0, 2)), "ctx", axis=1, tiled=True)

    moved = lax.all_to_all(loaded, "ctx", split_axis=1, concat_axis=0, tiled=True)
    slot_rows = moved.reshape(-1, moved.shape[3])
    targets = slot_pos.reshape(-1)
    picker = (targets[None, :] == jnp.arange(rows, dtype=jnp.int32)[:, None]).astype(bf16)
    own_part = jnp.dot(picker, slot_rows, preferred_element_type=f32).astype(bf16)
    tokens = gather_by_permutes(own_part, "fsdp", 1)

    proj = jnp.einsum("td,sdc->stc", tokens, weights, preferred_element_type=f32).astype(bf16)
    later_tokens, proj = lax.optimization_barrier((tokens, proj))
    gated_out, mixed, long_local, short_local = conv_block(
        proj, grad_out, short_taps, long_taps, contig_lengths
    )

    n_ctx = lax.axis_size("ctx")
    feats = tokens.shape[1] // n_ctx
    all_tokens = jnp.zeros((n_ctx * rows, feats), bf16)
    for source, piece in swap_by_permutes(later_tokens, "ctx", 1):
        all_tokens = lax.dynamic_update_slice_in_dim(all_tokens, piece, source * rows, 0)

    all_mixed = lax.all_gather(mixed, "ctx", axis=1, tiled=True)

    partial = jnp.einsum("stc,sdc->td", mixed, weights, preferred_element_type=f32).astype(bf16)
    token_grads = sum(
        piece.astype(f32) for _, piece in swap_by_permutes(partial, "fsdp", 1)
    ).astype(bf16)

    filter_grads = summed_over(
        jnp.concatenate([long_local, short_local.reshape(-1, chans)], 0), "ctx"
    )
    long_total = filter_grads[:long_w]
    short_total = filter_grads[long_w:].reshape(3, -1, chans)[:, :short_w]

    weight_grads = jnp.einsum(
        "td,stc->sdc", all_tokens, all_mixed, preferred_element_type=f32
    ).astype(bf16)
    return (
        gated_out, token_grads, jnp.transpose(weight_grads, (1, 0, 2)), short_total, long_total,
    )


def solution(mesh):
    in_specs = (
        P("ctx", None, None, "fsdp"),
        P("ctx", None, None),
        P(),
        P("ctx", None, "fsdp"),
        P(None, None, "fsdp"),
        P(None, "fsdp"),
        P("ctx", "fsdp"),
    )
    out_specs = (
        P("ctx", "fsdp"),
        P("ctx", "fsdp"),
        P("ctx", None, "fsdp"),
        P(None, None, "fsdp"),
        P(None, "fsdp"),
    )
    return jax.shard_map(
        on_device, mesh=mesh, in_specs=in_specs, out_specs=out_specs, check_vma=False
    )
```

```python
import jax
import jax.numpy as jnp
from jax import lax
from jax.experimental import pallas as pl
from jax.experimental.pallas import tpu as pltpu
from jax.sharding import PartitionSpec as P

LANES = 128


def round_up(x, to):
    return -(-x // to) * to


def neighbour_rows(x, axis, by):
    size = lax.axis_size(axis)
    pairs = [(i, i + by) for i in range(size) if 0 <= i + by < size]
    return lax.ppermute(x, axis, pairs)


def rotated(x, axis, by):
    size = lax.axis_size(axis)
    return lax.ppermute(x, axis, [(i, (i + by) % size) for i in range(size)])


def gather_by_permutes(x, axis, dim):
    size = lax.axis_size(axis)
    me = lax.axis_index(axis)
    width = x.shape[dim]
    shape = list(x.shape)
    shape[dim] = width * size
    out = lax.dynamic_update_slice_in_dim(jnp.zeros(shape, x.dtype), x, me * width, dim)
    for by in range(1, size):
        got = rotated(x, axis, by)
        out = lax.dynamic_update_slice_in_dim(out, got, ((me - by) % size) * width, dim)
    return out


def swap_by_permutes(x, axis, split_dim):
    size = lax.axis_size(axis)
    me = lax.axis_index(axis)
    width = x.shape[split_dim] // size
    pieces = [(me, lax.dynamic_slice_in_dim(x, me * width, width, split_dim))]
    for by in range(1, size):
        part = lax.dynamic_slice_in_dim(x, ((me + by) % size) * width, width, split_dim)
        pieces.append(((me - by) % size, rotated(part, axis, by)))
    return pieces


def summed_over(x, axis):
    size = lax.axis_size(axis)
    if size & (size - 1):
        return lax.psum(x.astype(jnp.bfloat16), axis).astype(jnp.float32)
    step = 1
    while step < size:
        mine = x.astype(jnp.bfloat16)
        got = lax.ppermute(mine, axis, [(i, i ^ step) for i in range(size)])
        x = mine.astype(jnp.float32) + got.astype(jnp.float32)
        step *= 2
    return x


def conv_kernel(
    dims, proj, prev12, prev0, next0, next12, grads, next_grads, dist, room, short, long,
    gated, mixed, long_sums, short_sums,
    s0, s1, s2, go, f0, f1, f2, prod, back, gf, acc,
):
    rows, lead, short_pad, short_w, long_w, tail = dims
    f32 = jnp.float32
    s0[0:short_pad, :] = prev0[...].astype(f32)
    s0[short_pad : short_pad + rows, :] = proj[0].astype(f32)
    s0[short_pad + rows :, :] = next0[...].astype(f32)
    for k, ref in ((0, s1), (1, s2)):
        ref[0 : lead + short_pad, :] = prev12[k].astype(f32)
        ref[lead + short_pad : lead + short_pad + rows, :] = proj[1 + k].astype(f32)
        ref[lead + short_pad + rows :, :] = next12[k].astype(f32)
    go[0:rows, :] = grads[...].astype(f32)
    go[rows:, :] = next_grads[...].astype(f32)

    def rounded(x):
        return x.astype(jnp.bfloat16).astype(f32)

    step = 8 * 7 if (lead + rows + tail) % 56 == 0 else 8

    def lead_short(ref, taps, base, reach, n):
        total = jnp.zeros((n, LANES), f32)
        for j in range(short_w):
            x = ref[pl.ds(base + short_pad - j, n), :]
            total = total + jnp.where(reach >= j, x, 0.0) * taps[j : j + 1, :]
        return total

    def before(i, _):
        base = pl.multiple_of(i * step, 8)
        reach = dist[pl.ds(base, step), :]
        a = lead_short(s1, short[1], base, reach, step)
        b = lead_short(s2, short[2], base, reach, step)
        f1[pl.ds(base, step), :] = a
        f2[pl.ds(base, step), :] = b
        prod[pl.ds(base, step), :] = rounded(a * b)
        return 0

    lax.fori_loop(0, (lead + rows + tail) // step, before, 0)

    def after(i, _):
        base = pl.multiple_of(i * step, 8)
        reach = dist[pl.ds(base + lead, step), :]
        a = lead_short(s0, short[0], base, reach, step)
        f0[pl.ds(base, step), :] = a
        back[pl.ds(base, step), :] = rounded(go[pl.ds(base, step), :] * a)
        return 0

    lax.fori_loop(0, (rows + tail + lead) // step, after, 0)

    acc[...] = jnp.zeros_like(acc)
    unroll = 8

    def long_tile(base, n, own):
        reach = dist[pl.ds(base + lead, n), :]
        ahead = room[pl.ds(base, n), :]
        here = back[pl.ds(base, n), :]

        def taps_step(i, carry):
            carried, grad = carry
            for u in range(unroll):
                j = i * unroll + u
                tap = long[pl.ds(j, 1), :]
                x = jnp.where(reach >= j, prod[pl.ds(base + lead - j, n), :], 0.0)
                y = jnp.where(ahead >= j, back[pl.ds(base + j, n), :], 0.0)
                carried = carried + x * tap
                grad = grad + y * tap
                if own:
                    z = here * x
                    part = z[0:8, :]
                    for r in range(8, n, 8):
                        part = part + z[r : r + 8, :]
                    at = pl.multiple_of(j * 8, 8)
                    acc[pl.ds(at, 8), :] += part
            return carried, grad

        zero = jnp.zeros((n, LANES), f32)
        carried, grad = lax.fori_loop(0, long_w // unroll, taps_step, (zero, zero))
        if own:
            gated[pl.ds(base, n), :] = (f0[pl.ds(base, n), :] * carried).astype(gated.dtype)
        gf[0, pl.ds(base, n), :] = rounded(go[pl.ds(base, n), :] * carried)
        gf[1, pl.ds(base, n), :] = rounded(grad * f2[pl.ds(base + lead, n), :])
        gf[2, pl.ds(base, n), :] = rounded(grad * f1[pl.ds(base + lead, n), :])

    tile = 64 if rows % 64 == 0 else 8
    lax.fori_loop(
        0, rows // tile, lambda i, _: (long_tile(pl.multiple_of(i * tile, 8), tile, True), 0)[1], 0
    )
    for extra in range(0, tail, 8):
        long_tile(rows + extra, 8, False)
    long_sums[...] = jnp.sum(acc[...].reshape(long_w, 8, LANES), axis=1)

    short_sums[...] = jnp.zeros_like(short_sums)

    def last(i, _):
        base = pl.multiple_of(i * tile, 8)
        reach = dist[pl.ds(base + lead, tile), :]
        ahead = room[pl.ds(base, tile), :]
        for s, ref, off in ((0, s0, 0), (1, s1, lead), (2, s2, lead)):
            total = jnp.zeros((tile, LANES), f32)
            here = gf[s, pl.ds(base, tile), :]
            for j in range(short_w):
                y = jnp.where(ahead >= j, gf[s, pl.ds(base + j, tile), :], 0.0)
                total = total + y * short[s, j : j + 1, :]
                x = jnp.where(reach >= j, ref[pl.ds(base + off + short_pad - j, tile), :], 0.0)
                short_sums[s, j : j + 1, :] += jnp.sum(here * x, axis=0, keepdims=True)
            mixed[s, pl.ds(base, tile), :] = total.astype(mixed.dtype)
        return 0

    lax.fori_loop(0, rows // tile, last, 0)


def conv_block(proj, grad_out, short_taps, long_taps, contig_lengths):
    _, rows, chans = proj.shape
    short_w, long_w = short_taps.shape[1], long_taps.shape[0]
    short_pad = 16
    lead = round_up(long_w, 16)
    tail = round_up(short_w - 1, 8)
    far = lead + short_pad

    up = neighbour_rows(proj[1:, rows - far :], "ctx", 1)
    up0 = neighbour_rows(proj[0, rows - short_pad :], "ctx", 1)
    down0 = neighbour_rows(proj[0, :far], "ctx", -1)
    down12 = neighbour_rows(proj[1:, :short_pad], "ctx", -1)
    down_grads = neighbour_rows(grad_out[:far], "ctx", -1)

    offset = lax.axis_index("ctx") * rows
    ends = jnp.cumsum(contig_lengths, dtype=jnp.int32)
    begins = ends - contig_lengths
    at = offset - lead + jnp.arange(lead + rows + far, dtype=jnp.int32)
    first = jnp.max(jnp.where(begins[None, :] <= at[:, None], begins[None, :], 0), axis=1)
    dist = jnp.broadcast_to((at - first)[:, None], (at.shape[0], LANES))
    here = offset + jnp.arange(rows + short_pad, dtype=jnp.int32)
    big = jnp.int32(2**30)
    end = jnp.min(jnp.where(ends[None, :] > here[:, None], ends[None, :], big), axis=1)
    room = jnp.broadcast_to((end - 1 - here)[:, None], (here.shape[0], LANES))

    def block(*lead_dims):
        n = len(lead_dims)
        return pl.BlockSpec((*lead_dims, LANES), lambda i: (0,) * n + (i,))

    def whole(r):
        return pl.BlockSpec((r, LANES), lambda i: (0, 0))

    def vmem(*shape):
        return pltpu.VMEM((*shape, LANES), jnp.float32)

    span = lead + rows + tail
    dims = (rows, lead, short_pad, short_w, long_w, tail)
    return pl.pallas_call(
        lambda *refs: conv_kernel(dims, *refs),
        grid=(chans // LANES,),
        in_specs=[
            block(3, rows), block(2, far), block(short_pad), block(far), block(2, short_pad),
            block(rows), block(far), whole(dist.shape[0]), whole(room.shape[0]),
            block(3, short_w), block(long_w),
        ],
        out_specs=[block(rows), block(3, rows), block(long_w), block(3, 8 * -(-short_w // 8))],
        out_shape=[
            jax.ShapeDtypeStruct((rows, chans), jnp.bfloat16),
            jax.ShapeDtypeStruct((3, rows, chans), jnp.bfloat16),
            jax.ShapeDtypeStruct((long_w, chans), jnp.float32),
            jax.ShapeDtypeStruct((3, 8 * -(-short_w // 8), chans), jnp.float32),
        ],
        scratch_shapes=[
            vmem(short_pad + rows + far), vmem(far + rows + short_pad),
            vmem(far + rows + short_pad), vmem(rows + far),
            vmem(span), vmem(span), vmem(span), vmem(span), vmem(span),
            vmem(3, rows + short_pad), vmem(long_w * 8),
        ],
        compiler_params=pltpu.CompilerParams(vmem_limit_bytes=40 << 20),
        cost_estimate=pl.CostEstimate(
            flops=rows * chans * long_w * 10, bytes_accessed=rows * chans * 24, transcendentals=0
        ),
        name="hyena_filters",
    )(proj, up, up0, down0, down12, grad_out, down_grads, dist, room, short_taps, long_taps)


def weight_kernel(tokens_t, grads, *rest):
    rest[-1][...] = jnp.dot(
        tokens_t[...], grads[...], preferred_element_type=jnp.float32
    ).astype(jnp.bfloat16)


def weight_part(tokens_t, grads, before, part, chans):
    feats, count = tokens_t.shape
    streams, _, width = grads.shape
    more = () if before is None else (before,)
    return pl.pallas_call(
        weight_kernel,
        grid=(streams,),
        in_specs=[
            pl.BlockSpec((feats, count), lambda s: (0, 0)),
            pl.BlockSpec((None, count, width), lambda s: (s, 0, 0)),
        ] + [pl.BlockSpec(memory_space=pl.ANY) for _ in more],
        out_specs=pl.BlockSpec((None, feats, width), lambda s: (s, 0, part)),
        out_shape=jax.ShapeDtypeStruct((streams, feats, chans), jnp.bfloat16),
        input_output_aliases={2: 0} if more else {},
        compiler_params=pltpu.CompilerParams(vmem_limit_bytes=58 << 20),
        cost_estimate=pl.CostEstimate(
            flops=2 * feats * count * streams * width,
            bytes_accessed=2 * streams * width * (count + feats) + 2 * feats * count,
            transcendentals=0,
        ),
        name="weight_grads",
    )(tokens_t, grads, *more)


def on_device(loaded, slot_pos, contig_lengths, w_in, short_taps, long_taps, grad_out):
    f32, bf16 = jnp.float32, jnp.bfloat16
    rows, chans = grad_out.shape
    short_w, long_w = short_taps.shape[1], long_taps.shape[0]
    parts = 2 if chans % (2 * LANES) == 0 else 1
    width = chans // parts
    cuts = [slice(p * width, (p + 1) * width) for p in range(parts)]

    by_stream = jnp.transpose(w_in, (1, 0, 2))
    weights = [lax.all_gather(by_stream[:, :, c], "ctx", axis=1, tiled=True) for c in cuts]

    moved = lax.all_to_all(loaded, "ctx", split_axis=1, concat_axis=0, tiled=True)
    slot_rows = moved.reshape(-1, moved.shape[3])
    targets = slot_pos.reshape(-1)
    picker = (targets[None, :] == jnp.arange(rows, dtype=jnp.int32)[:, None]).astype(bf16)
    own_part = jnp.dot(picker, slot_rows, preferred_element_type=f32).astype(bf16)
    tokens = gather_by_permutes(own_part, "fsdp", 1)

    gated, mixed, gathered, sums = [], [], [], []
    partial = None
    pieces = swap_by_permutes(tokens, "ctx", 1)
    sources = [source for source, _ in pieces]
    pieces = [piece for _, piece in pieces]
    for p, c in enumerate(cuts):
        held = weights[p]
        if p:
            held, mixed[-1], partial = lax.optimization_barrier((held, mixed[-1], partial))
        proj = jnp.einsum("td,sdc->stc", tokens, held, preferred_element_type=f32).astype(bf16)
        out, grads, long_local, short_local = conv_block(
            proj, grad_out[:, c], short_taps[:, :, c], long_taps[:, c], contig_lengths
        )
        if p == 0:
            grads, *pieces = lax.optimization_barrier((grads, *pieces))
        gated.append(out)
        mixed.append(grads)
        sums.append(jnp.concatenate([long_local, short_local.reshape(-1, width)], 0))
        gathered.append(lax.all_gather(grads, "ctx", axis=1, tiled=True))
        term = jnp.einsum("stc,sdc->td", grads, held, preferred_element_type=f32)
        partial = term if partial is None else partial + term
    token_grads = sum(
        piece.astype(f32) for _, piece in swap_by_permutes(partial.astype(bf16), "fsdp", 1)
    ).astype(bf16)

    filter_grads = summed_over(jnp.concatenate(sums, 1), "ctx")
    long_total = filter_grads[:long_w]
    short_total = filter_grads[long_w:].reshape(3, -1, chans)[:, :short_w]

    n_ctx = lax.axis_size("ctx")
    tokens_t = jnp.zeros((tokens.shape[1] // n_ctx, n_ctx * rows), bf16)
    for source, piece in zip(sources, pieces):
        tokens_t = lax.dynamic_update_slice_in_dim(tokens_t, piece.T, source * rows, 1)
    weight_grads = None
    for p, g in enumerate(gathered):
        weight_grads = weight_part(tokens_t, g, weight_grads, p, chans)
    return (
        jnp.concatenate(gated, 1), token_grads, jnp.transpose(weight_grads, (1, 0, 2)), short_total, long_total,
    )


def solution(mesh):
    in_specs = (
        P("ctx", None, None, "fsdp"),
        P("ctx", None, None),
        P(),
        P("ctx", None, "fsdp"),
        P(None, None, "fsdp"),
        P(None, "fsdp"),
        P("ctx", "fsdp"),
    )
    out_specs = (
        P("ctx", "fsdp"),
        P("ctx", "fsdp"),
        P("ctx", None, "fsdp"),
        P(None, None, "fsdp"),
        P(None, "fsdp"),
    )
    return jax.shard_map(
        on_device, mesh=mesh, in_specs=in_specs, out_specs=out_specs, check_vma=False
    )
```
